32 devices in a mesh: grid: 8 (over y, x, core), pts: 4 (over z).
Axes of the slice: x: 2, y: 2, z: 4, core: 2. Of those that a mesh axis runs over, the one named last changes fastest.
Arguments:
- phi_blocks: bfloat16 [8, 6, 3200, 512], P('grid'), may hold values from -0.0546875 to 0.0546875
- phi_points: bfloat16 [8, 3200, 2048], P('grid', None, 'pts'), may hold values from -6 to 6
- tile_mask: int32 [8, 6, 4], P('grid', None, 'pts'), may hold values 0 or 1
- support: int32 [8, 6], P('grid'), may hold values from 0 to 7, as said below
- point_order: int32 [2048], replicated, may hold values from 0 to 2047, each once
- gram_inverse: bfloat16 [2048, 2048], P('pts'), may hold values from -0.125 to 0.125
Outputs:
- fitted: bfloat16 [2048, 4096], P('pts', 'grid')
The draws below stay inside these ranges and needn't reach their ends.
Inputs may be any that keep to these rules, and one draw needn't show every extreme that they name: `support`: each row holds 6 distinct slab indices, the first the row's own slab, the others within 3 slabs of it, counted cyclically.
All inputs are finite; a program needn't handle non-finite values. No bound on the sum of `tile_mask` on one device may be relied on, other than what follows from the above.
Results may differ from the reference program's by a relative error of at most 0.005.
Values sent between devices are 32-bit elements; how exact they have to be, the bound alone decides.
No kernel may reach another device: no remote copies, remote signals or barrier semaphores. Data moves between devices by JAX's collectives and lax.ppermute only.
A program may use at most 128 MiB of HBM per device.

```python
import jax
import jax.numpy as jnp
from jax import lax

CELLS = 512
ORBS = 3200
BATCH = 512
SUPPORT = 6
REACH = 3
POINTS = 2048
GRIDPTS = 4096
N_GRID = 8
N_PTS = 4


def draw_support(key, part):
    row_keys = jax.random.split(key, N_GRID)
    candidates = jnp.concatenate([jnp.arange(-REACH, 0, dtype=jnp.int32), jnp.arange(1, REACH + 1, dtype=jnp.int32)])

    def one_row(row_key):
        return jax.random.permutation(row_key, candidates)[:SUPPORT - 1]
    chosen = jax.vmap(one_row)(row_keys)
    offsets = jnp.concatenate([jnp.zeros((N_GRID, 1), jnp.int32), chosen.astype(jnp.int32)], axis=1)
    owners = jnp.arange(N_GRID, dtype=jnp.int32)[:, None]
    return ((owners + offsets) % N_GRID).astype(jnp.int32)


def plant(values, key, low, top_value):
    index_at = [jax.random.randint(jax.random.fold_in(key, axis), (), 0, length) for axis, length in enumerate(values.shape)]
    main_axis = values.shape.index(max(values.shape))
    next_to = index_at[:main_axis] + [(index_at[main_axis] + 1) % values.shape[main_axis]] + index_at[main_axis + 1:]
    return values.at[tuple(index_at)].set(low).at[tuple(next_to)].set(top_value)


def block_scale(own_key, shape, cuts, low, high):
    def one(position, parts):
        draws = jax.random.uniform(jax.random.fold_in(jax.random.fold_in(own_key, 6), position), (parts,), jnp.float32, low / len(cuts), high / len(cuts))
        return jnp.repeat(jnp.exp(draws), shape[position] // parts).reshape((-1,) + (1,) * (len(shape) - position - 1))

    loudness = one(*cuts[0])
    for cut in cuts[1:]:
        loudness = loudness * one(*cut)
    return loudness


def noise(key, dims, scale, bound, cuts=(), kind=jnp.bfloat16):
    drawn = jax.random.normal(key, dims, jnp.float32) * scale
    if len(cuts) > 0:
        drawn = block_scale(key, dims, cuts, -0.22, 0.18) * drawn
    return jnp.clip(drawn, min=-bound, max=bound).astype(kind)


def setup_inputs(seed: int = 0) -> dict:
    seeds = jax.random.split(jax.random.key(seed), 7)
    return {
        "phi_blocks": noise(seeds[0], (N_GRID, SUPPORT, ORBS, CELLS), (4 * ORBS) ** -0.5, 0.0546875, ((0, 8),)),
        "phi_points": noise(seeds[1], (N_GRID, ORBS, POINTS), 1.0, 6.0, ((0, 8), (2, 4))),
        "tile_mask": plant((jax.random.randint(seeds[2], (N_GRID, SUPPORT, N_PTS), 0, 3) < 2).astype(jnp.int32), jax.random.fold_in(seeds[2], 1), 0, 1),
        "support": draw_support(jax.random.fold_in(seeds[6], 71), 0),
        "point_order": jax.random.permutation(seeds[4], POINTS).astype(jnp.int32),
        "gram_inverse": noise(seeds[5], (POINTS, POINTS), POINTS ** -0.5, 0.125, ((0, 4),)),
    }


def reference(phi_blocks, phi_points, tile_mask, support, point_order, gram_inverse):
    def add_tile(step_index, pair_field):
        owner_slab = step_index // SUPPORT
        block_index = step_index % SUPPORT
        tile_term = jnp.dot(phi_points[owner_slab].T, phi_blocks[owner_slab, block_index], preferred_element_type=jnp.float32)
        row_mask = jnp.repeat(tile_mask[owner_slab, block_index], BATCH, total_repeat_length=POINTS).astype(jnp.float32)
        column_start = (support[owner_slab, block_index] * CELLS).astype(jnp.int32)
        anchor = jnp.zeros((), jnp.int32)
        current = lax.dynamic_slice(pair_field, (anchor, column_start), (POINTS, CELLS))
        return lax.dynamic_update_slice(pair_field, current + tile_term * row_mask[:, None], (anchor, column_start))

    pair_field = lax.fori_loop(0, N_GRID * SUPPORT, add_tile, jnp.zeros((POINTS, GRIDPTS), jnp.float32))
    squared = (pair_field * pair_field).astype(jnp.bfloat16)
    columns = gram_inverse[:, point_order]
    return jnp.dot(columns.T, squared, preferred_element_type=jnp.float32).astype(jnp.bfloat16)
```

```python
import functools

import jax
import jax.numpy as jnp
from jax import lax
from jax.experimental import pallas as pl
from jax.experimental.pallas import tpu as pltpu
from jax.sharding import PartitionSpec as P

REACH = 3
F32 = jnp.float32


def turned_kernel(points_ref, turned_ref):
    turned_ref[...] = points_ref[...].T


def turned(points):
    orbs, batch = points.shape
    step = 640
    return pl.pallas_call(
        turned_kernel,
        grid=(orbs // step,),
        in_specs=[pl.BlockSpec((step, batch), lambda i: (i, 0))],
        out_specs=pl.BlockSpec((batch, step), lambda i: (0, i)),
        out_shape=jax.ShapeDtypeStruct((batch, orbs), points.dtype),
        cost_estimate=pl.CostEstimate(flops=0, bytes_accessed=4 * orbs * batch, transcendentals=0),
        name="turned",
    )(points)


def products_kernel(block_of, live, points_ref, blocks_ref, out_ref):
    del block_of
    place = pl.program_id(0)

    @pl.when(live[place] != 0)
    def _():
        out_ref[0] = jnp.dot(points_ref[...], blocks_ref[0], preferred_element_type=F32)

    @pl.when(live[place] == 0)
    def _():
        out_ref[...] = jnp.zeros_like(out_ref)


def products(points, blocks, block_of, live, places, column, width):
    batch, orbs = points.shape
    count = len(places)
    block_of = jnp.concatenate([block_of[p : p + 1] for p in places] + [jnp.zeros((8,), jnp.int32)])
    live = jnp.concatenate([live[p : p + 1] for p in places] + [jnp.zeros((8,), jnp.int32)])
    return pl.pallas_call(
        products_kernel,
        grid_spec=pltpu.PrefetchScalarGridSpec(
            num_scalar_prefetch=2,
            grid=(count,),
            in_specs=[
                pl.BlockSpec((batch, orbs), lambda i, block_of, live: (0, 0), pipeline_mode=pl.Buffered(1)),
                pl.BlockSpec((1, orbs, width), lambda i, block_of, live: (block_of[i], 0, column)),
            ],
            out_specs=pl.BlockSpec((1, batch, width), lambda i, block_of, live: (i, 0, 0)),
        ),
        out_shape=jax.ShapeDtypeStruct((count, batch, width), F32),
        cost_estimate=pl.CostEstimate(
            flops=2 * count * batch * orbs * width,
            bytes_accessed=2 * orbs * (batch + count * width) + 4 * count * batch * width,
            transcendentals=0,
        ),
        name="products",
    )(block_of, live, points, blocks)


def picked_kernel(order_ref, gram_ref, out_ref):
    rows, points = order_ref.shape[0], gram_ref.shape[1]
    lanes = lax.broadcasted_iota(jnp.int32, (rows, points), 1)
    chosen = (lanes == order_ref[...]).astype(gram_ref.dtype)
    out_ref[...] = lax.dot_general(
        chosen, gram_ref[...], (((1,), (1,)), ((), ())), preferred_element_type=F32
    ).astype(out_ref.dtype)


def picked(gram, point_order):
    batch, points = gram.shape
    rows = 256
    return pl.pallas_call(
        picked_kernel,
        grid=(points // rows,),
        in_specs=[
            pl.BlockSpec((rows, 1), lambda i: (i, 0)),
            pl.BlockSpec((batch, points), lambda i: (0, 0), pipeline_mode=pl.Buffered(1)),
        ],
        out_specs=pl.BlockSpec((rows, batch), lambda i: (i, 0)),
        out_shape=jax.ShapeDtypeStruct((points, batch), gram.dtype),
        cost_estimate=pl.CostEstimate(
            flops=2 * points * points * batch, bytes_accessed=4 * batch * points, transcendentals=0
        ),
        name="picked",
    )(point_order[:, None], gram)


def shares_kernel(me, columns_ref, *refs):
    *terms, out_ref, squared = refs

    @pl.when(pl.program_id(0) == 0)
    def _():
        field = sum(t[...] for t in terms[1:]) + terms[0][...]
        squared[...] = (field * field).astype(squared.dtype)

    out_ref[0] = jnp.dot(columns_ref[...], squared[...], preferred_element_type=F32)


def shares(me, columns, terms):
    batch, width = terms[0].shape
    count = columns.shape[0] // batch
    return pl.pallas_call(
        shares_kernel,
        grid_spec=pltpu.PrefetchScalarGridSpec(
            num_scalar_prefetch=1,
            grid=(count,),
            in_specs=[pl.BlockSpec((batch, batch), lambda i, me: (lax.rem(me[0] + i, count), 0))]
            + [pl.BlockSpec((batch, width), lambda i, me: (0, 0))] * len(terms),
            out_specs=pl.BlockSpec((1, batch, width), lambda i, me: (i, 0, 0)),
            scratch_shapes=[pltpu.VMEM((batch, width), columns.dtype)],
        ),
        out_shape=jax.ShapeDtypeStruct((count, batch, width), F32),
        cost_estimate=pl.CostEstimate(
            flops=2 * count * batch * batch * width,
            bytes_accessed=2 * count * batch * batch + 4 * (count + len(terms)) * batch * width,
            transcendentals=0,
        ),
        name="shares",
    )(me, columns, *terms)


def swapped(block, mask, count):
    return lax.ppermute(block, "grid", [(i, i ^ mask) for i in range(count)])


def passed_along(block, distance, count):
    return lax.ppermute(block, "grid", [((i - distance) % count, i) for i in range(count)])


def on_device(phi_blocks, phi_points, tile_mask, support, point_order, gram_inverse):
    slabs, batches = lax.axis_size("grid"), lax.axis_size("pts")
    own_slab, own_batch = lax.axis_index("grid"), lax.axis_index("pts")
    blocks = phi_blocks[0]
    cube = slabs == 8
    if cube:
        targets = own_slab ^ jnp.arange(8, dtype=jnp.int32)
    else:
        targets = (own_slab + jnp.arange(-REACH, REACH + 1, dtype=jnp.int32)) % slabs
    match = targets[:, None] == support[0][None, :]
    block_of = jnp.sum(jnp.where(match, jnp.arange(support.shape[1], dtype=jnp.int32)[None, :], 0), axis=1)
    live = jnp.sum(jnp.where(match, tile_mask[0, :, 0][None, :], 0), axis=1)
    points = turned(phi_points[0])
    columns = picked(gram_inverse, point_order)
    me = own_batch.astype(jnp.int32)[None]
    cells = phi_blocks.shape[-1]
    width = 256

    fitted = []
    for part in range(cells // width):
        make = functools.partial(products, points, blocks, block_of, live, column=part, width=width)
        if cube:
            first, second = (2, 4) if part % 2 == 0 else (4, 2)
            away = make(places=[1, 3, 5, 7])
            came = swapped(away, 1, slabs)
            held = make(places=[0, 2, 6])
            near = {0: held[0] + came[0], 2: held[1] + came[1], 4: came[2], 6: held[2] + came[3]}
            sent = jnp.stack([near[first], near[6]])
            got = swapped(sent, first, slabs)
            onward = near[second] + got[1]
            last = swapped(onward, second, slabs)
            terms = [near[0], got[0], last]
        else:
            tiles = make(places=list(range(2 * REACH + 1)))
            terms = [tiles[REACH]] + [
                passed_along(tiles[REACH + d], d, slabs) for d in range(-REACH, REACH + 1) if d != 0
            ]
        share = shares(me, columns, terms)
        up = down = None
        for step in range(1, batches):
            up = share[batches - step] if up is None else up + share[batches - step]
            down = share[step] if down is None else down + share[step]
            up = lax.ppermute(up, "pts", [(i, i + 1) for i in range(step)])
            down = lax.ppermute(down, "pts", [(batches - 1 - i, batches - 2 - i) for i in range(step)])
        fitted.append((share[0] + up + down).astype(jnp.bfloat16))
    return jnp.concatenate(fitted, axis=1)


def solution(mesh):
    in_specs = (
        P("grid", None, None, None),
        P("grid", None, "pts"),
        P("grid", None, "pts"),
        P("grid", None),
        P(),
        P("pts", None),
    )
    out_specs = P("pts", "grid")
    return jax.shard_map(
        on_device, mesh=mesh, in_specs=in_specs, out_specs=out_specs, check_vma=False
    )
```

```python
import functools

import jax
import jax.numpy as jnp
from jax import lax
from jax.experimental import pallas as pl
from jax.experimental.pallas import tpu as pltpu
from jax.sharding import PartitionSpec as P

REACH = 3
F32 = jnp.float32
WIDTHS = (128, 128, 256)
ORDER = (0, 2, 1)
HOLD = {0: (), 2: ((0, 0),), 1: ((0, 1),)}


def lasting(us):
    return pl.CostEstimate(flops=int(us * 1e9), bytes_accessed=int(us * 3e6), transcendentals=0)


CHUNKS = 4


def product(points_ref, block):
    return lax.dot_general(points_ref[...], block, (((0,), (0,)), ((), ())), preferred_element_type=F32)


def fetched_kernel(count, block_of, live, points_ref, blocks_hbm, out_ref, slots, done):
    rows = slots.shape[1] // CHUNKS

    def copies(n):
        return [
            pltpu.make_async_copy(
                blocks_hbm.at[block_of[n], pl.ds(c * rows, rows)], slots.at[n % 2, pl.ds(c * rows, rows)], done.at[n % 2, c]
            )
            for c in range(CHUNKS)
        ]

    def start(n):
        @pl.when(live[n] != 0)
        def _():
            for copy in copies(n):
                copy.start()

    start(0)
    for n in range(count):

        @pl.when(live[n] != 0)
        def _(n=n):
            for copy in copies(n):
                copy.wait()

        if n + 1 < count:
            start(n + 1)

        @pl.when(live[n] != 0)
        def _(n=n):
            out_ref[n] = product(points_ref, slots[n % 2])

        @pl.when(live[n] == 0)
        def _(n=n):
            out_ref[n] = jnp.zeros(out_ref.shape[1:], F32)


SMEM = pl.BlockSpec(memory_space=pltpu.SMEM)
VMEM = pl.BlockSpec(memory_space=pltpu.VMEM)


def params(mib):
    return pltpu.CompilerParams(vmem_limit_bytes=mib << 20)


def fetched(points, blocks, block_of, live, count):
    orbs, batch = points.shape
    cells = blocks.shape[2]
    return pl.pallas_call(
        functools.partial(fetched_kernel, count),
        in_specs=[SMEM, SMEM, VMEM, pl.BlockSpec(memory_space=pltpu.HBM)],
        out_specs=VMEM,
        out_shape=jax.ShapeDtypeStruct((count, batch, cells), F32),
        scratch_shapes=[pltpu.VMEM((2, orbs, cells), blocks.dtype), pltpu.SemaphoreType.DMA((2, CHUNKS))],
        compiler_params=params(16),
        cost_estimate=lasting(2.5 * count),
        name="fetched",
    )(block_of, live, in_vmem(points), blocks)


def held_kernel(base, block_of, live, points_ref, blocks_ref, *outs):
    for n, out in enumerate(outs):

        @pl.when(live[base + n] != 0)
        def _(n=n, out=out):
            out[...] = product(points_ref, blocks_ref[block_of[base + n]])

        @pl.when(live[base + n] == 0)
        def _(out=out):
            out[...] = jnp.zeros(out.shape, F32)


def held(points, blocks, block_of, live, base, count):
    batch, cells = points.shape[1], blocks.shape[2]
    return pl.pallas_call(
        functools.partial(held_kernel, base),
        in_specs=[SMEM, SMEM, VMEM, VMEM],
        out_specs=[VMEM] * count,
        out_shape=[jax.ShapeDtypeStruct((batch, cells), F32)] * count,
        compiler_params=params(8),
        cost_estimate=lasting(2.0 * count),
        name="held",
    )(block_of, live, in_vmem(points), in_vmem(blocks))


def near_kernel(base, widths, block_of, live, points_ref, blocks_ref, came_ref, *outs):
    pieces = len(widths)

    def put(n, value):
        start = 0
        for out, width in zip(outs[n * pieces : (n + 1) * pieces], widths):
            out[...] = value[:, start : start + width]
            start += width

    for n in range(2):

        @pl.when(live[base + n] != 0)
        def _(n=n):
            put(n, product(points_ref, blocks_ref[block_of[base + n]]) + came_ref[n])

        @pl.when(live[base + n] == 0)
        def _(n=n):
            put(n, came_ref[n])

    put(2, came_ref[2])


def near_sums(points, blocks, block_of, live, base, came, widths):
    batch = points.shape[1]
    return pl.pallas_call(
        functools.partial(near_kernel, base, widths),
        in_specs=[SMEM, SMEM, VMEM, VMEM, VMEM],
        out_specs=[pl.BlockSpec((batch, width), lambda i: (0, 0)) for _ in range(3) for width in widths],
        out_shape=[pltpu.HBM((batch, width), F32) for _ in range(3) for width in widths],
        grid=(1,),
        compiler_params=params(12),
        cost_estimate=lasting(5.0),
        name="near_sums",
    )(block_of, live, in_vmem(points), in_vmem(blocks), in_vmem(came))


def in_vmem(array):
    return pltpu.with_memory_space_constraint(array, pltpu.VMEM)


def picked_kernel(order_ref, gram_ref, out_ref):
    points, columns = gram_ref.shape[1], order_ref.shape[1]
    rows = lax.broadcasted_iota(jnp.int32, (points, columns), 0)
    chosen = (rows == order_ref[...]).astype(gram_ref.dtype)
    out_ref[...] = jnp.dot(gram_ref[...], chosen, preferred_element_type=F32).astype(out_ref.dtype)


def picked(gram, point_order):
    batch, points = gram.shape
    columns = 256
    return pl.pallas_call(
        picked_kernel,
        grid=(points // columns,),
        in_specs=[
            pl.BlockSpec((1, columns), lambda i: (0, i)),
            pl.BlockSpec((batch, points), lambda i: (0, 0), pipeline_mode=pl.Buffered(1)),
        ],
        out_specs=pl.BlockSpec((batch, columns), lambda i: (0, i)),
        out_shape=jax.ShapeDtypeStruct((batch, points), gram.dtype),
        compiler_params=pltpu.CompilerParams(vmem_limit_bytes=24 << 20),
        cost_estimate=lasting(8.0),
        name="picked",
    )(point_order[None, :], gram)


def shares_kernel(pieces, count, me, columns_ref, *refs):
    terms, outs, squared = refs[: -count - 1], refs[-count - 1 : -1], refs[-1]

    @pl.when(pl.program_id(0) == 0)
    def _():
        at = start = 0
        for number, width in pieces:
            field = terms[at][...]
            for t in terms[at + 1 : at + number]:
                field = field + t[...]
            squared[:, start : start + width] = (field * field).astype(squared.dtype)
            at, start = at + number, start + width

    share = lax.dot_general(columns_ref[...], squared[...], (((0,), (0,)), ((), ())), preferred_element_type=F32)
    for n in range(count):

        @pl.when(pl.program_id(0) == n)
        def _(n=n):
            outs[n][...] = share


def shares(me, columns, pieces):
    batch = pieces[0][1][0][0].shape[-2]
    count = columns.shape[1] // batch
    in_specs = [pl.BlockSpec((batch, batch), lambda i, me: (0, lax.rem(me[0] + i, count)))]
    args = []
    for width, terms in pieces:
        for array, at in terms:
            lead = (pl.Squeezed(),) * (array.ndim - 2)
            in_specs.append(pl.BlockSpec((*lead, batch, width), lambda i, me, at=at: at, pipeline_mode=pl.Buffered(1)))
            args.append(array)
    total = sum(width for width, _ in pieces)
    return pl.pallas_call(
        functools.partial(shares_kernel, tuple((len(terms), width) for width, terms in pieces), count),
        grid_spec=pltpu.PrefetchScalarGridSpec(
            num_scalar_prefetch=1,
            grid=(count,),
            in_specs=in_specs,
            out_specs=[pl.BlockSpec((batch, total), lambda i, me: (0, 0))] * count,
            scratch_shapes=[pltpu.VMEM((batch, total), columns.dtype)],
        ),
        out_shape=[jax.ShapeDtypeStruct((batch, total), F32)] * count,
        compiler_params=pltpu.CompilerParams(vmem_limit_bytes=24 << 20),
        cost_estimate=lasting(5.0),
        name="shares",
    )(me, columns, *args)


def swapped(block, mask, count):
    return lax.ppermute(block, "grid", [(i, i ^ mask) for i in range(count)])


def passed_along(block, distance, count):
    return lax.ppermute(block, "grid", [((i - distance) % count, i) for i in range(count)])


def combined(share, batches):
    up = down = None
    links = []
    for step in range(1, batches):
        up = share[batches - step] if up is None else up + share[batches - step]
        down = share[step] if down is None else down + share[step]
        up = lax.ppermute(up, "pts", [(i, i + 1) for i in range(step)])
        down = lax.ppermute(down, "pts", [(batches - 1 - i, batches - 2 - i) for i in range(step)])
        links.append((up, down))
    return (share[0] + up + down).astype(jnp.bfloat16), links


def after(value, *others):
    return lax.optimization_barrier((value, *others))[0]


def on_device(phi_blocks, phi_points, tile_mask, support, point_order, gram_inverse):
    slabs, batches = lax.axis_size("grid"), lax.axis_size("pts")
    own_slab, own_batch = lax.axis_index("grid"), lax.axis_index("pts")
    blocks = phi_blocks[0]
    cube = slabs == 8
    if cube:
        targets = own_slab ^ jnp.array([3, 7, 5, 0, 1, 2, 6, 0] + [0] * 8, jnp.int32)
    else:
        targets = (own_slab + jnp.array([d % slabs for d in range(-REACH, REACH + 1)] + [0] * 9, jnp.int32)) % slabs
    match = targets[:, None] == support[0][None, :]
    block_of = jnp.sum(jnp.where(match, jnp.arange(support.shape[1], dtype=jnp.int32)[None, :], 0), axis=1)
    live = jnp.sum(jnp.where(match, tile_mask[0, :, 0][None, :], 0), axis=1)
    me = own_batch.astype(jnp.int32)[None]
    cells = phi_blocks.shape[-1]
    points = phi_points[0]
    if cube:
        away = fetched(points, pltpu.with_memory_space_constraint(blocks, pltpu.HBM), block_of, live, 3)
        came = swapped(away, 1, slabs)
        blocks = in_vmem(blocks)
        own, other = held(after(points, away), blocks, block_of, live, 3, 2)
        near = near_sums(after(points, own), blocks, block_of, live, 5, came, WIDTHS)
        late = swapped(after(other, near[0]), 1, slabs)
        columns = picked(after(gram_inverse, (near[0], late)), point_order)
        pieces, links, got = {}, {}, None
        for n in ORDER:
            width = WIDTHS[n]
            at = sum(WIDTHS[:n]) // width
            sums = [near[place * len(WIDTHS) + n] for place in range(3)]
            if got is not None:
                sums = [after(block, (before, late)) for block, before in zip(sums, got)]
            got = [swapped(block, mask, slabs) for block, mask in zip(sums, (2, 6, 4))]
            pending = [links[p][step] for p, step in HOLD[n]]
            if pending:
                columns = after(columns, pending)
            piece = (width, [(own, (0, at)), (late, (0, at))] + [(block, (0, 0)) for block in got])
            share = shares(me, columns, [piece])
            columns = after(columns, share[0])
            pieces[n], links[n] = combined(share, batches)
        fitted = [pieces[n] for n in range(len(WIDTHS))]
    else:
        tiles = fetched(points, pltpu.with_memory_space_constraint(blocks, pltpu.HBM), block_of, live, 2 * REACH + 1)
        columns = picked(gram_inverse, point_order)
        piece = (cells, [(tiles, (REACH, 0, 0))] + [
            (passed_along(tiles[REACH + d], d, slabs), (0, 0)) for d in range(-REACH, REACH + 1) if d != 0
        ])
        fitted = [combined(shares(me, columns, [piece]), batches)[0]]
    return jnp.concatenate(fitted, axis=1)


def solution(mesh):
    in_specs = (
        P("grid", None, None, None),
        P("grid", None, "pts"),
        P("grid", None, "pts"),
        P("grid", None),
        P(),
        P("pts", None),
    )
    out_specs = P("pts", "grid")
    return jax.shard_map(
        on_device, mesh=mesh, in_specs=in_specs, out_specs=out_specs, check_vma=False
    )
```

```python
import functools

import jax
import jax.numpy as jnp
from jax import lax
from jax.experimental import pallas as pl
from jax.experimental.pallas import tpu as pltpu
from jax.sharding import PartitionSpec as P

REACH = 3
F32 = jnp.float32
WIDTHS = (128, 128, 128, 128)
ORDER = (0, 1, 2, 3)
HOLD = {0: (), 1: (), 2: ((0, 0),), 3: ((1, 0), (0, 1))}
AFTER = (None, None, 0, 1)


def lasting(us):
    return pl.CostEstimate(flops=int(us * 1e9), bytes_accessed=int(us * 3e6), transcendentals=0)


CHUNKS = 4


def product(points_ref, block):
    return lax.dot_general(points_ref[...], block, (((0,), (0,)), ((), ())), preferred_element_type=F32)


def fetched_kernel(count, block_of, live, points_ref, blocks_hbm, out_ref, slots, done):
    rows = slots.shape[1] // CHUNKS

    def copies(n):
        return [
            pltpu.make_async_copy(
                blocks_hbm.at[block_of[n], pl.ds(c * rows, rows)], slots.at[n % 2, pl.ds(c * rows, rows)], done.at[n % 2, c]
            )
            for c in range(CHUNKS)
        ]

    def start(n):
        @pl.when(live[n] != 0)
        def _():
            for copy in copies(n):
                copy.start()

    start(0)
    for n in range(count):

        @pl.when(live[n] != 0)
        def _(n=n):
            for copy in copies(n):
                copy.wait()

        if n + 1 < count:
            start(n + 1)

        @pl.when(live[n] != 0)
        def _(n=n):
            out_ref[n] = product(points_ref, slots[n % 2])

        @pl.when(live[n] == 0)
        def _(n=n):
            out_ref[n] = jnp.zeros(out_ref.shape[1:], F32)


SMEM = pl.BlockSpec(memory_space=pltpu.SMEM)
VMEM = pl.BlockSpec(memory_space=pltpu.VMEM)


def params(mib):
    return pltpu.CompilerParams(vmem_limit_bytes=mib << 20)


def fetched(points, blocks, block_of, live, count):
    orbs, batch = points.shape
    cells = blocks.shape[2]
    return pl.pallas_call(
        functools.partial(fetched_kernel, count),
        in_specs=[SMEM, SMEM, VMEM, pl.BlockSpec(memory_space=pltpu.HBM)],
        out_specs=VMEM,
        out_shape=jax.ShapeDtypeStruct((count, batch, cells), F32),
        scratch_shapes=[pltpu.VMEM((2, orbs, cells), blocks.dtype), pltpu.SemaphoreType.DMA((2, CHUNKS))],
        compiler_params=params(16),
        cost_estimate=lasting(2.5 * count),
        name="fetched",
    )(block_of, live, in_vmem(points), blocks)


def held_kernel(base, block_of, live, points_ref, blocks_ref, *outs):
    for n, out in enumerate(outs):

        @pl.when(live[base + n] != 0)
        def _(n=n, out=out):
            out[...] = product(points_ref, blocks_ref[block_of[base + n]])

        @pl.when(live[base + n] == 0)
        def _(out=out):
            out[...] = jnp.zeros(out.shape, F32)


def held(points, blocks, block_of, live, base, count):
    batch, cells = points.shape[1], blocks.shape[2]
    return pl.pallas_call(
        functools.partial(held_kernel, base),
        in_specs=[SMEM, SMEM, VMEM, VMEM],
        out_specs=[VMEM] * count,
        out_shape=[jax.ShapeDtypeStruct((batch, cells), F32)] * count,
        compiler_params=params(8),
        cost_estimate=lasting(2.0 * count),
        name="held",
    )(block_of, live, in_vmem(points), in_vmem(blocks))


def near_kernel(base, widths, block_of, live, points_ref, blocks_ref, came_ref, *outs):
    pieces = len(widths)

    def put(n, value):
        start = 0
        for out, width in zip(outs[n * pieces : (n + 1) * pieces], widths):
            out[...] = value[:, start : start + width]
            start += width

    for n in range(2):

        @pl.when(live[base + n] != 0)
        def _(n=n):
            put(n, product(points_ref, blocks_ref[block_of[base + n]]) + came_ref[n])

        @pl.when(live[base + n] == 0)
        def _(n=n):
            put(n, came_ref[n])

    put(2, came_ref[2])


def near_sums(points, blocks, block_of, live, base, came, widths):
    batch = points.shape[1]
    return pl.pallas_call(
        functools.partial(near_kernel, base, widths),
        in_specs=[SMEM, SMEM, VMEM, VMEM, VMEM],
        out_specs=[pl.BlockSpec((batch, width), lambda i: (0, 0)) for _ in range(3) for width in widths],
        out_shape=[pltpu.HBM((batch, width), F32) for _ in range(3) for width in widths],
        grid=(1,),
        compiler_params=params(12),
        cost_estimate=lasting(5.0),
        name="near_sums",
    )(block_of, live, in_vmem(points), in_vmem(blocks), in_vmem(came))


def in_vmem(array):
    return pltpu.with_memory_space_constraint(array, pltpu.VMEM)


def picked_kernel(order_ref, gram_ref, out_ref):
    points, columns = gram_ref.shape[1], order_ref.shape[1]
    rows = lax.broadcasted_iota(jnp.int32, (points, columns), 0)
    chosen = (rows == order_ref[...]).astype(gram_ref.dtype)
    out_ref[...] = jnp.dot(gram_ref[...], chosen, preferred_element_type=F32).astype(out_ref.dtype)


def picked(gram, point_order):
    batch, points = gram.shape
    columns = 256
    return pl.pallas_call(
        picked_kernel,
        grid=(points // columns,),
        in_specs=[
            pl.BlockSpec((1, columns), lambda i: (0, i)),
            pl.BlockSpec((batch, points), lambda i: (0, 0), pipeline_mode=pl.Buffered(1)),
        ],
        out_specs=pl.BlockSpec((batch, columns), lambda i: (0, i)),
        out_shape=jax.ShapeDtypeStruct((batch, points), gram.dtype),
        compiler_params=pltpu.CompilerParams(vmem_limit_bytes=24 << 20),
        cost_estimate=lasting(8.0),
        name="picked",
    )(point_order[None, :], gram)


def shares_kernel(pieces, count, me, columns_ref, *refs):
    terms, outs, squared = refs[: -count // 2 - 2], refs[-count // 2 - 2 : -1], refs[-1]

    @pl.when(pl.program_id(0) == 0)
    def _():
        at = start = 0
        for number, width in pieces:
            field = terms[at][...]
            for t in terms[at + 1 : at + number]:
                field = field + t[...]
            squared[:, start : start + width] = (field * field).astype(squared.dtype)
            at, start = at + number, start + width

    share = lax.dot_general(columns_ref[...], squared[...], (((0,), (0,)), ((), ())), preferred_element_type=F32)
    half = count // 2
    for n in range(half):

        @pl.when(pl.program_id(0) == n)
        def _(n=n):
            outs[0][n] = share

        @pl.when(pl.program_id(0) == half + n)
        def _(n=n):
            outs[1 + n][...] = share


def shares(me, columns, pieces):
    batch = pieces[0][1][0][0].shape[-2]
    count = columns.shape[1] // batch
    half = count // 2

    def turn(i, me):
        return 0, me[0] ^ jnp.where(i < half, 2 * i + 1, jnp.minimum(2 * (i - half), count - 2))

    in_specs = [pl.BlockSpec((batch, batch), turn)]
    args = []
    for width, terms in pieces:
        for array, at in terms:
            lead = (pl.Squeezed(),) * (array.ndim - 2)
            in_specs.append(pl.BlockSpec((*lead, batch, width), lambda i, me, at=at: at, pipeline_mode=pl.Buffered(1)))
            args.append(array)
    total = sum(width for width, _ in pieces)
    return pl.pallas_call(
        functools.partial(shares_kernel, tuple((len(terms), width) for width, terms in pieces), count),
        grid_spec=pltpu.PrefetchScalarGridSpec(
            num_scalar_prefetch=1,
            grid=(count,),
            in_specs=in_specs,
            out_specs=[pl.BlockSpec((half, batch, total), lambda i, me: (0, 0, 0))]
            + [pl.BlockSpec((batch, total), lambda i, me: (0, 0))] * half,
            scratch_shapes=[pltpu.VMEM((batch, total), columns.dtype)],
        ),
        out_shape=[jax.ShapeDtypeStruct((half, batch, total), F32)] + [jax.ShapeDtypeStruct((batch, total), F32)] * half,
        compiler_params=params(24),
        cost_estimate=lasting(3.0),
        name="shares",
    )(me, columns, *args)


def swapped(block, mask, count):
    return lax.ppermute(block, "grid", [(i, i ^ mask) for i in range(count)])


def passed_along(block, distance, count):
    return lax.ppermute(block, "grid", [((i - distance) % count, i) for i in range(count)])


def combined(share, batches):
    sent, kept, links = share[0], list(share[1:]), []
    distance = 1
    while distance < batches:
        came = lax.ppermute(sent, "pts", [(i, i ^ distance) for i in range(batches)])
        links.append(came)
        kept = [block + came[n] for n, block in enumerate(kept)]
        if len(kept) > 1:
            sent, kept = kept[1::2], kept[0::2]
            sent = jnp.stack(sent) if len(sent) > 1 else sent[0][None]
        distance *= 2
    return kept[0].astype(jnp.bfloat16), links


def after(value, *others):
    return lax.optimization_barrier((value, *others))[0]


def on_device(phi_blocks, phi_points, tile_mask, support, point_order, gram_inverse):
    slabs, batches = lax.axis_size("grid"), lax.axis_size("pts")
    own_slab, own_batch = lax.axis_index("grid"), lax.axis_index("pts")
    blocks = phi_blocks[0]
    cube = slabs == 8
    if cube:
        targets = own_slab ^ jnp.array([3, 7, 5, 0, 1, 2, 6, 0] + [0] * 8, jnp.int32)
    else:
        targets = (own_slab + jnp.array([d % slabs for d in range(-REACH, REACH + 1)] + [0] * 9, jnp.int32)) % slabs
    match = targets[:, None] == support[0][None, :]
    block_of = jnp.sum(jnp.where(match, jnp.arange(support.shape[1], dtype=jnp.int32)[None, :], 0), axis=1)
    live = jnp.sum(jnp.where(match, tile_mask[0, :, 0][None, :], 0), axis=1)
    me = own_batch.astype(jnp.int32)[None]
    cells = phi_blocks.shape[-1]
    points = phi_points[0]
    if cube:
        away = fetched(points, pltpu.with_memory_space_constraint(blocks, pltpu.HBM), block_of, live, 3)
        came = swapped(away, 1, slabs)
        blocks = in_vmem(blocks)
        own, other = held(after(points, away), blocks, block_of, live, 3, 2)
        near = near_sums(after(points, own), blocks, block_of, live, 5, came, WIDTHS)
        late = swapped(after(other, near[0]), 1, slabs)
        columns = picked(after(gram_inverse, (near[0], late)), point_order)
        pieces, links, gots = {}, {}, {}
        for n in ORDER:
            width = WIDTHS[n]
            at = sum(WIDTHS[:n]) // width
            sums = [near[place * len(WIDTHS) + n] for place in range(3)]
            if AFTER[n] is not None:
                sums = [after(block, (before, late)) for block, before in zip(sums, gots[AFTER[n]])]
            got = gots[n] = [swapped(block, mask, slabs) for block, mask in zip(sums, (2, 6, 4))]
            pending = [links[p][step] for p, step in HOLD[n]]
            if pending:
                columns = after(columns, pending)
            piece = (width, [(own, (0, at)), (late, (0, at))] + [(block, (0, 0)) for block in got])
            share = shares(me, columns, [piece])
            columns = after(columns, share[0])
            pieces[n], links[n] = combined(share, batches)
        fitted = [pieces[n] for n in range(len(WIDTHS))]
    else:
        tiles = fetched(points, pltpu.with_memory_space_constraint(blocks, pltpu.HBM), block_of, live, 2 * REACH + 1)
        columns = picked(gram_inverse, point_order)
        piece = (cells, [(tiles, (REACH, 0, 0))] + [
            (passed_along(tiles[REACH + d], d, slabs), (0, 0)) for d in range(-REACH, REACH + 1) if d != 0
        ])
        fitted = [combined(shares(me, columns, [piece]), batches)[0]]
    return jnp.concatenate(fitted, axis=1)


def solution(mesh):
    in_specs = (
        P("grid", None, None, None),
        P("grid", None, "pts"),
        P("grid", None, "pts"),
        P("grid", None),
        P(),
        P("pts", None),
    )
    out_specs = P("pts", "grid")
    return jax.shard_map(
        on_device, mesh=mesh, in_specs=in_specs, out_specs=out_specs, check_vma=False
    )
```

```python
import functools

import jax
import jax.numpy as jnp
from jax import lax
from jax.experimental import pallas as pl
from jax.experimental.pallas import tpu as pltpu
from jax.sharding import PartitionSpec as P

REACH = 3
F32 = jnp.float32
WIDTHS = (128, 128, 128, 128)
ORDER = (0, 1, 2, 3)
HOLD = {0: (), 1: (), 2: ((0, 1),), 3: ((0, 1),)}
AFTER = ((), (), (('got', 0),), (('got', 1), ('squared', 0)))


def lasting(us):
    return pl.CostEstimate(flops=int(us * 1e9), bytes_accessed=int(us * 3e6), transcendentals=0)


CHUNKS = 4


def product(points_ref, block):
    return lax.dot_general(points_ref[...], block, (((0,), (0,)), ((), ())), preferred_element_type=F32)


def stream(block_of, live, points_ref, blocks_hbm, slots, done, base, count, emit):
    rows = slots.shape[1] // CHUNKS

    def copies(n):
        return [
            pltpu.make_async_copy(
                blocks_hbm.at[block_of[base + n], pl.ds(c * rows, rows)],
                slots.at[n % 2, pl.ds(c * rows, rows)],
                done.at[n % 2, c],
            )
            for c in range(CHUNKS)
        ]

    def start(n):
        @pl.when(live[base + n] != 0)
        def _():
            for copy in copies(n):
                copy.start()

    start(0)
    for n in range(count):

        @pl.when(live[base + n] != 0)
        def _(n=n):
            for copy in copies(n):
                copy.wait()

        if n + 1 < count:
            start(n + 1)

        @pl.when(live[base + n] != 0)
        def _(n=n):
            emit(n, product(points_ref, slots[n % 2]))

        @pl.when(live[base + n] == 0)
        def _(n=n):
            emit(n, None)


def fetched_kernel(count, block_of, live, points_ref, blocks_hbm, out_ref, slots, done):
    def emit(n, term):
        out_ref[n] = jnp.zeros(out_ref.shape[1:], F32) if term is None else term

    stream(block_of, live, points_ref, blocks_hbm, slots, done, 0, count, emit)


HBM = pl.BlockSpec(memory_space=pltpu.HBM)
SMEM = pl.BlockSpec(memory_space=pltpu.SMEM)
VMEM = pl.BlockSpec(memory_space=pltpu.VMEM)


def slots_for(blocks):
    return [pltpu.VMEM((2, *blocks.shape[1:]), blocks.dtype), pltpu.SemaphoreType.DMA((2, CHUNKS))]


def params(mib):
    return pltpu.CompilerParams(vmem_limit_bytes=mib << 20)


def fetched(points, blocks, block_of, live, count):
    orbs, batch = points.shape
    cells = blocks.shape[2]
    return pl.pallas_call(
        functools.partial(fetched_kernel, count),
        in_specs=[SMEM, SMEM, VMEM, pl.BlockSpec(memory_space=pltpu.HBM)],
        out_specs=VMEM,
        out_shape=jax.ShapeDtypeStruct((count, batch, cells), F32),
        scratch_shapes=slots_for(blocks),
        compiler_params=params(10),
        cost_estimate=lasting(2.5 * count),
        name="fetched",
    )(block_of, live, in_vmem(points), blocks)


def held_kernel(base, block_of, live, points_ref, blocks_hbm, *refs):
    *outs, slots, done = refs

    def emit(n, term):
        outs[n][...] = jnp.zeros(outs[n].shape, F32) if term is None else term

    stream(block_of, live, points_ref, blocks_hbm, slots, done, base, len(outs), emit)


def held(points, blocks, block_of, live, base, count):
    batch, cells = points.shape[1], blocks.shape[2]
    return pl.pallas_call(
        functools.partial(held_kernel, base),
        in_specs=[SMEM, SMEM, VMEM, HBM],
        out_specs=[VMEM] * count,
        out_shape=[jax.ShapeDtypeStruct((batch, cells), F32)] * count,
        scratch_shapes=slots_for(blocks),
        compiler_params=params(10),
        cost_estimate=lasting(2.0 * count),
        name="held",
    )(block_of, live, in_vmem(points), blocks)


def near_kernel(base, widths, block_of, live, points_ref, blocks_hbm, came_ref, *refs):
    *outs, slots, done = refs
    pieces = len(widths)

    def put(n, value):
        start = 0
        for out, width in zip(outs[n * pieces : (n + 1) * pieces], widths):
            out[...] = value[:, start : start + width]
            start += width

    put(2, came_ref[2])

    def emit(n, term):
        put(n, came_ref[n] if term is None else term + came_ref[n])

    stream(block_of, live, points_ref, blocks_hbm, slots, done, base, 2, emit)


def near_sums(points, blocks, block_of, live, base, came, widths):
    batch = points.shape[1]
    return pl.pallas_call(
        functools.partial(near_kernel, base, widths),
        in_specs=[SMEM, SMEM, VMEM, HBM, VMEM],
        scratch_shapes=slots_for(blocks),
        out_specs=[pl.BlockSpec((batch, width), lambda i: (0, 0)) for _ in range(3) for width in widths],
        out_shape=[pltpu.HBM((batch, width), F32) for _ in range(3) for width in widths],
        grid=(1,),
        compiler_params=params(16),
        cost_estimate=lasting(5.0),
        name="near_sums",
    )(block_of, live, in_vmem(points), blocks, in_vmem(came))


def in_vmem(array):
    return pltpu.with_memory_space_constraint(array, pltpu.VMEM)


def picked_kernel(where, order_ref, gram_ref, out_ref):
    del where
    rows = lax.broadcasted_iota(jnp.int32, (gram_ref.shape[1], order_ref.shape[1]), 0)
    chosen = (rows == order_ref[...]).astype(gram_ref.dtype)
    out_ref[...] = jnp.dot(gram_ref[...], chosen, preferred_element_type=F32).astype(out_ref.dtype)


def picked(where, gram, point_order, given):
    batch, points = gram.shape
    rows, span = batch // 2 if given else batch, 256
    per = batch // span

    def turn(i, where):
        return 0, (where[0] ^ (2 * lax.div(i, per) + given)) * per + lax.rem(i, per)

    return pl.pallas_call(
        picked_kernel,
        grid_spec=pltpu.PrefetchScalarGridSpec(
            num_scalar_prefetch=1,
            grid=(points // 2 // span,),
            in_specs=[
                pl.BlockSpec((1, span), turn),
                pl.BlockSpec(
                    (rows, points), lambda i, where: (where[1] if given else 0, 0), pipeline_mode=pl.Buffered(1)
                ),
            ],
            out_specs=pl.BlockSpec((rows, span), lambda i, where: (0, i)),
        ),
        out_shape=jax.ShapeDtypeStruct((rows, points // 2), F32 if given else gram.dtype),
        compiler_params=params(12),
        cost_estimate=lasting(3.0),
        name="picked",
    )(where, point_order[None, :], gram)


def joined_kernel(where, mine_ref, other_ref, out_ref):
    rows = mine_ref.shape[0]

    @pl.when(where[1] == 0)
    def _():
        out_ref[:rows] = mine_ref[...].astype(out_ref.dtype)
        out_ref[rows:] = other_ref[...].astype(out_ref.dtype)

    @pl.when(where[1] != 0)
    def _():
        out_ref[rows:] = mine_ref[...].astype(out_ref.dtype)
        out_ref[:rows] = other_ref[...].astype(out_ref.dtype)


def joined(where, mine, other):
    rows, columns = mine.shape
    return pl.pallas_call(
        joined_kernel,
        in_specs=[SMEM, VMEM, VMEM],
        out_specs=VMEM,
        out_shape=jax.ShapeDtypeStruct((2 * rows, columns), jnp.bfloat16),
        compiler_params=params(8),
        cost_estimate=lasting(1.5),
        name="joined",
    )(where, mine, other)


def squares_kernel(*refs):
    field = refs[0][...]
    for term in refs[1:-1]:
        field = field + term[...]
    refs[-1][...] = (field * field).astype(jnp.bfloat16).astype(F32)


def squares(width, terms):
    batch = terms[0][0].shape[-2]
    in_specs = []
    for array, at in terms:
        lead = (pl.Squeezed(),) * (array.ndim - 2)
        in_specs.append(pl.BlockSpec((*lead, batch, width), lambda i, at=at: at))
    return pl.pallas_call(
        squares_kernel,
        grid=(1,),
        in_specs=in_specs,
        out_specs=pl.BlockSpec((batch, width), lambda i: (0, 0)),
        out_shape=jax.ShapeDtypeStruct((batch, width), F32),
        compiler_params=params(8),
        cost_estimate=lasting(1.5),
        name="squares",
    )(*[array for array, _ in terms])


def shares_kernel(kept_ref, joined_ref, own_ref, came_ref, *outs):
    own, came = own_ref[...].astype(kept_ref.dtype), came_ref[...].astype(kept_ref.dtype)
    batch = own.shape[0]
    for n, out in enumerate(outs):
        cut = slice(n * batch, (n + 1) * batch)
        out[...] = lax.dot_general(
            kept_ref[:, cut], own, (((0,), (0,)), ((), ())), preferred_element_type=F32
        ) + lax.dot_general(joined_ref[:, cut], came, (((0,), (0,)), ((), ())), preferred_element_type=F32)


def shares(kept, joined, own, came):
    batch, width = own.shape
    count = kept.shape[1] // batch
    return pl.pallas_call(
        shares_kernel,
        in_specs=[VMEM] * 4,
        out_specs=[VMEM] * count,
        out_shape=[jax.ShapeDtypeStruct((batch, width), F32)] * count,
        compiler_params=params(8),
        cost_estimate=lasting(2.0),
        name="shares",
    )(kept, joined, own, came)


def swapped(block, mask, count):
    return lax.ppermute(block, "grid", [(i, i ^ mask) for i in range(count)])


def passed_along(block, distance, count):
    return lax.ppermute(block, "grid", [((i - distance) % count, i) for i in range(count)])


def turned(block, distance, count):
    return lax.ppermute(block, "pts", [(i, i ^ distance) for i in range(count)])


def combined(share, batches):
    kept, links = list(share), []
    distance = 2
    while distance < batches:
        sent, kept = kept[1::2], kept[0::2]
        came = turned(jnp.stack(sent) if len(sent) > 1 else sent[0][None], distance, batches)
        links.append(came)
        kept = [block + came[n] for n, block in enumerate(kept)]
        distance *= 2
    return kept[0].astype(jnp.bfloat16), links


def after(value, *others):
    return lax.optimization_barrier((value, *others))[0]


def on_device(phi_blocks, phi_points, tile_mask, support, point_order, gram_inverse):
    slabs, batches = lax.axis_size("grid"), lax.axis_size("pts")
    own_slab, own_batch = lax.axis_index("grid"), lax.axis_index("pts")
    blocks = pltpu.with_memory_space_constraint(phi_blocks[0], pltpu.HBM)
    cube = slabs == 8
    if cube:
        targets = own_slab ^ jnp.array([3, 7, 5, 0, 1, 2, 6, 0] + [0] * 8, jnp.int32)
    else:
        targets = (own_slab + jnp.array([d % slabs for d in range(-REACH, REACH + 1)] + [0] * 9, jnp.int32)) % slabs
    match = targets[:, None] == support[0][None, :]
    block_of = jnp.sum(jnp.where(match, jnp.arange(support.shape[1], dtype=jnp.int32)[None, :], 0), axis=1)
    live = jnp.sum(jnp.where(match, tile_mask[0, :, 0][None, :], 0), axis=1)
    where = jnp.stack([own_batch, own_slab & 1]).astype(jnp.int32)
    cells = phi_blocks.shape[-1]
    points = phi_points[0]
    if cube:
        away = fetched(points, blocks, block_of, live, 3)
        came = swapped(away, 1, slabs)
        own, other = held(after(points, away), blocks, block_of, live, 3, 2)
        theirs = turned(picked(where, after(gram_inverse, own), point_order, 1), 1, batches)
        near = near_sums(after(points, own), blocks, block_of, live, 5, came, WIDTHS)
        pieces, links, gots, squared = {}, {}, {}, {}
        columns = None
        for n in ORDER:
            width = WIDTHS[n]
            at = sum(WIDTHS[:n]) // width
            sums = [near[place * len(WIDTHS) + n] for place in range(3)]
            if n == ORDER[1]:
                sums = after(sums, late)
            if AFTER[n]:
                sums = after(sums, [{"got": gots, "squared": squared, "sum": links}[kind][p] for kind, p in AFTER[n]])
            got = gots[n] = [swapped(block, mask, slabs) for block, mask in zip(sums, (2, 6, 4))]
            if columns is None:
                late = swapped(after(other, near), 1, slabs)
                theirs = after(theirs, got)
                columns = joined(where, theirs, swapped(theirs, 1, slabs))
            terms = [(own, (0, at)), (late, (0, at))] + [(block, (0, 0)) for block in got]
            mine = squares(width, terms)
            squared[n] = turned(mine, 1, batches)
            if n == ORDER[0]:
                kept = picked(where, after(gram_inverse, near), point_order, 0)
            pending = [links[p][0] if step else squared[p] for p, step in HOLD[n]]
            if pending:
                kept = after(kept, pending)
            share = shares(kept, columns, mine, squared[n])
            kept = after(kept, share[0])
            pieces[n], links[n] = combined(share, batches)
        fitted = [pieces[n] for n in range(len(WIDTHS))]
    else:
        tiles = fetched(points, blocks, block_of, live, 2 * REACH + 1)
        kept = picked(where, gram_inverse, point_order, 0)
        theirs = turned(picked(where, gram_inverse, point_order, 1), 1, batches)
        columns = joined(where, theirs, swapped(theirs, 1, slabs))
        terms = [(tiles, (REACH, 0, 0))] + [
            (passed_along(tiles[REACH + d], d, slabs), (0, 0)) for d in range(-REACH, REACH + 1) if d != 0
        ]
        mine = squares(cells, terms)
        fitted = [combined(shares(kept, columns, mine, turned(mine, 1, batches)), batches)[0]]
    return jnp.concatenate(fitted, axis=1)


def solution(mesh):
    in_specs = (
        P("grid", None, None, None),
        P("grid", None, "pts"),
        P("grid", None, "pts"),
        P("grid", None),
        P(),
        P("pts", None),
    )
    out_specs = P("pts", "grid")
    return jax.shard_map(
        on_device, mesh=mesh, in_specs=in_specs, out_specs=out_specs, check_vma=False
    )
```

```python
import functools

import jax
import jax.numpy as jnp
from jax import lax
from jax.experimental import pallas as pl
from jax.experimental.pallas import tpu as pltpu
from jax.sharding import PartitionSpec as P

REACH = 3
F32 = jnp.float32
WIDTHS = (128, 128, 128, 128)
ORDER = (0, 1, 2, 3)
HOLD = {0: (), 1: (), 2: ((0, 1),), 3: ((0, 1),)}
AFTER = ((), (), (('got', 0),), (('got', 1), ('squared', 0)))


def lasting(us):
    return pl.CostEstimate(flops=int(us * 1e9), bytes_accessed=int(us * 3e6), transcendentals=0)


CHUNKS = 4


def product(points_ref, block):
    return lax.dot_general(points_ref[...], block, (((0,), (0,)), ((), ())), preferred_element_type=F32)


def stream(block_of, live, points_ref, blocks_hbm, slots, done, base, count, emit, before=None, behind=None):
    rows = slots.shape[1] // CHUNKS

    def copies(n):
        return [
            pltpu.make_async_copy(
                blocks_hbm.at[block_of[base + n], pl.ds(c * rows, rows)],
                slots.at[n % 2, pl.ds(c * rows, rows)],
                done.at[n % 2, c],
            )
            for c in range(CHUNKS)
        ]

    def start(n):
        @pl.when(live[base + n] != 0)
        def _():
            for copy in copies(n):
                copy.start()

    start(0)
    for n in range(count):

        @pl.when(live[base + n] != 0)
        def _(n=n):
            for copy in copies(n):
                copy.wait()

        if n + 1 < count:
            start(n + 1)

        if before:
            before(n)

        @pl.when(live[base + n] != 0)
        def _(n=n):
            emit(n, product(points_ref, slots[n % 2]))

        @pl.when(live[base + n] == 0)
        def _(n=n):
            emit(n, None)

        if behind:
            behind(n)


def fetched_kernel(count, block_of, live, points_ref, blocks_hbm, out_hbm, slots, done, stage, sent):
    def copy(n):
        return pltpu.make_async_copy(stage.at[n % 2], out_hbm.at[n], sent.at[n % 2])

    def before(n):
        if n >= 2:
            copy(n - 2).wait()

    def emit(n, term):
        stage[n % 2] = jnp.zeros(stage.shape[1:], F32) if term is None else term

    def behind(n):
        copy(n).start()

    stream(block_of, live, points_ref, blocks_hbm, slots, done, 0, count, emit, before, behind)
    for n in range(max(count - 2, 0), count):
        copy(n).wait()


HBM = pl.BlockSpec(memory_space=pltpu.HBM)
SMEM = pl.BlockSpec(memory_space=pltpu.SMEM)
VMEM = pl.BlockSpec(memory_space=pltpu.VMEM)


def slots_for(blocks):
    return [pltpu.VMEM((2, *blocks.shape[1:]), blocks.dtype), pltpu.SemaphoreType.DMA((2, CHUNKS))]


def params(mib):
    return pltpu.CompilerParams(vmem_limit_bytes=mib << 20)


def fetched(points, blocks, block_of, live, count):
    orbs, batch = points.shape
    cells = blocks.shape[2]
    return pl.pallas_call(
        functools.partial(fetched_kernel, count),
        in_specs=[SMEM, SMEM, VMEM, pl.BlockSpec(memory_space=pltpu.HBM)],
        out_specs=HBM,
        out_shape=jax.ShapeDtypeStruct((count, batch, cells), F32),
        scratch_shapes=slots_for(blocks)
        + [pltpu.VMEM((2, batch, cells), F32), pltpu.SemaphoreType.DMA((2,))],
        compiler_params=params(10),
        cost_estimate=lasting(2.5 * count),
        name="fetched",
    )(block_of, live, in_vmem(points), blocks)


def held_kernel(base, block_of, live, points_ref, blocks_hbm, *refs):
    *outs, slots, done = refs

    def emit(n, term):
        outs[n][...] = jnp.zeros(outs[n].shape, F32) if term is None else term

    stream(block_of, live, points_ref, blocks_hbm, slots, done, base, len(outs), emit)


def held(points, blocks, block_of, live, base, count):
    batch, cells = points.shape[1], blocks.shape[2]
    return pl.pallas_call(
        functools.partial(held_kernel, base),
        in_specs=[SMEM, SMEM, VMEM, HBM],
        out_specs=[VMEM] * count,
        out_shape=[jax.ShapeDtypeStruct((batch, cells), F32)] * count,
        scratch_shapes=slots_for(blocks),
        compiler_params=params(10),
        cost_estimate=lasting(2.0 * count),
        name="held",
    )(block_of, live, in_vmem(points), blocks)


def near_kernel(base, widths, block_of, live, points_ref, blocks_hbm, came_ref, *refs):
    *outs, slots, done = refs
    pieces = len(widths)

    def put(n, value):
        start = 0
        for out, width in zip(outs[n * pieces : (n + 1) * pieces], widths):
            out[...] = value[:, start : start + width]
            start += width

    put(2, came_ref[2])

    def emit(n, term):
        put(n, came_ref[n] if term is None else term + came_ref[n])

    stream(block_of, live, points_ref, blocks_hbm, slots, done, base, 2, emit)


def near_sums(points, blocks, block_of, live, base, came, widths):
    batch = points.shape[1]
    return pl.pallas_call(
        functools.partial(near_kernel, base, widths),
        in_specs=[SMEM, SMEM, VMEM, HBM, VMEM],
        scratch_shapes=slots_for(blocks),
        out_specs=[pl.BlockSpec((batch, width), lambda i: (0, 0)) for _ in range(3) for width in widths],
        out_shape=[pltpu.HBM((batch, width), F32) for _ in range(3) for width in widths],
        grid=(1,),
        compiler_params=params(16),
        cost_estimate=lasting(5.0),
        name="near_sums",
    )(block_of, live, in_vmem(points), blocks, in_vmem(came))


def in_vmem(array):
    return pltpu.with_memory_space_constraint(array, pltpu.VMEM)


def picked_kernel(where, order_ref, gram_ref, out_ref):
    del where
    rows = lax.broadcasted_iota(jnp.int32, (gram_ref.shape[1], order_ref.shape[1]), 0)
    chosen = (rows == order_ref[...]).astype(gram_ref.dtype)
    out_ref[...] = jnp.dot(gram_ref[...], chosen, preferred_element_type=F32).astype(out_ref.dtype)


def picked(where, gram, point_order, given):
    batch, points = gram.shape
    rows, span = batch // 2 if given else batch, 256
    per = batch // span

    def turn(i, where):
        return 0, (where[0] ^ (2 * lax.div(i, per) + given)) * per + lax.rem(i, per)

    return pl.pallas_call(
        picked_kernel,
        grid_spec=pltpu.PrefetchScalarGridSpec(
            num_scalar_prefetch=1,
            grid=(points // 2 // span,),
            in_specs=[
                pl.BlockSpec((1, span), turn),
                pl.BlockSpec(
                    (rows, points), lambda i, where: (where[1] if given else 0, 0), pipeline_mode=pl.Buffered(1)
                ),
            ],
            out_specs=pl.BlockSpec((rows, span), lambda i, where: (0, i)),
        ),
        out_shape=jax.ShapeDtypeStruct((rows, points // 2), F32 if given else gram.dtype),
        compiler_params=params(12),
        cost_estimate=lasting(3.0),
        name="picked",
    )(where, point_order[None, :], gram)


def joined_kernel(where, mine_ref, other_ref, out_ref):
    rows = mine_ref.shape[0]

    @pl.when(where[1] == 0)
    def _():
        out_ref[:rows] = mine_ref[...].astype(out_ref.dtype)
        out_ref[rows:] = other_ref[...].astype(out_ref.dtype)

    @pl.when(where[1] != 0)
    def _():
        out_ref[rows:] = mine_ref[...].astype(out_ref.dtype)
        out_ref[:rows] = other_ref[...].astype(out_ref.dtype)


def joined(where, mine, other):
    rows, columns = mine.shape
    return pl.pallas_call(
        joined_kernel,
        in_specs=[SMEM, VMEM, VMEM],
        out_specs=VMEM,
        out_shape=jax.ShapeDtypeStruct((2 * rows, columns), jnp.bfloat16),
        compiler_params=params(8),
        cost_estimate=lasting(1.5),
        name="joined",
    )(where, mine, other)


def squares_kernel(*refs):
    field = refs[0][...]
    for term in refs[1:-1]:
        field = field + term[...]
    refs[-1][...] = (field * field).astype(jnp.bfloat16).astype(F32)


def squares(width, terms):
    batch = terms[0][0].shape[-2]
    in_specs = []
    for array, at in terms:
        lead = (pl.Squeezed(),) * (array.ndim - 2)
        in_specs.append(pl.BlockSpec((*lead, batch, width), lambda i, at=at: at))
    return pl.pallas_call(
        squares_kernel,
        grid=(1,),
        in_specs=in_specs,
        out_specs=pl.BlockSpec((batch, width), lambda i: (0, 0)),
        out_shape=jax.ShapeDtypeStruct((batch, width), F32),
        compiler_params=params(8),
        cost_estimate=lasting(1.5),
        name="squares",
    )(*[array for array, _ in terms])


def shares_kernel(kept_ref, joined_ref, own_ref, came_ref, *outs):
    own, came = own_ref[...].astype(kept_ref.dtype), came_ref[...].astype(kept_ref.dtype)
    batch = own.shape[0]
    for n, out in enumerate(outs):
        cut = slice(n * batch, (n + 1) * batch)
        out[...] = lax.dot_general(
            kept_ref[:, cut], own, (((0,), (0,)), ((), ())), preferred_element_type=F32
        ) + lax.dot_general(joined_ref[:, cut], came, (((0,), (0,)), ((), ())), preferred_element_type=F32)


def shares(kept, joined, own, came):
    batch, width = own.shape
    count = kept.shape[1] // batch
    return pl.pallas_call(
        shares_kernel,
        in_specs=[VMEM] * 4,
        out_specs=[VMEM] * count,
        out_shape=[jax.ShapeDtypeStruct((batch, width), F32)] * count,
        compiler_params=params(8),
        cost_estimate=lasting(2.0),
        name="shares",
    )(kept, joined, own, came)


def swapped(block, mask, count):
    return lax.ppermute(block, "grid", [(i, i ^ mask) for i in range(count)])


def passed_along(block, distance, count):
    return lax.ppermute(block, "grid", [((i - distance) % count, i) for i in range(count)])


def turned(block, distance, count):
    return lax.ppermute(block, "pts", [(i, i ^ distance) for i in range(count)])


def combined(share, batches):
    kept, links = list(share), []
    distance = 2
    while distance < batches:
        sent, kept = kept[1::2], kept[0::2]
        came = turned(jnp.stack(sent) if len(sent) > 1 else sent[0][None], distance, batches)
        links.append(came)
        kept = [block + came[n] for n, block in enumerate(kept)]
        distance *= 2
    return kept[0].astype(jnp.bfloat16), links


def after(value, *others):
    return lax.optimization_barrier((value, *others))[0]


def on_device(phi_blocks, phi_points, tile_mask, support, point_order, gram_inverse):
    slabs, batches = lax.axis_size("grid"), lax.axis_size("pts")
    own_slab, own_batch = lax.axis_index("grid"), lax.axis_index("pts")
    blocks = pltpu.with_memory_space_constraint(phi_blocks[0], pltpu.HBM)
    cube = slabs == 8
    if cube:
        targets = own_slab ^ jnp.array([3, 7, 5, 0, 1, 2, 6, 0] + [0] * 8, jnp.int32)
    else:
        targets = (own_slab + jnp.array([d % slabs for d in range(-REACH, REACH + 1)] + [0] * 9, jnp.int32)) % slabs
    match = targets[:, None] == support[0][None, :]
    block_of = jnp.sum(jnp.where(match, jnp.arange(support.shape[1], dtype=jnp.int32)[None, :], 0), axis=1)
    live = jnp.sum(jnp.where(match, tile_mask[0, :, 0][None, :], 0), axis=1)
    where = jnp.stack([own_batch, own_slab & 1]).astype(jnp.int32)
    cells = phi_blocks.shape[-1]
    points = phi_points[0]
    if cube:
        away = fetched(points, blocks, block_of, live, 3)
        came = swapped(away, 1, slabs)
        own, other = held(after(points, away), blocks, block_of, live, 3, 2)
        theirs = turned(picked(where, after(gram_inverse, own), point_order, 1), 1, batches)
        near = near_sums(after(points, own), blocks, block_of, live, 5, came, WIDTHS)
        pieces, links, gots, squared = {}, {}, {}, {}
        columns = None
        for n in ORDER:
            width = WIDTHS[n]
            at = sum(WIDTHS[:n]) // width
            sums = [near[place * len(WIDTHS) + n] for place in range(3)]
            if n == ORDER[1]:
                sums = after(sums, late)
            if AFTER[n]:
                sums = after(sums, [{"got": gots, "squared": squared, "sum": links}[kind][p] for kind, p in AFTER[n]])
            got = gots[n] = [swapped(block, mask, slabs) for block, mask in zip(sums, (2, 6, 4))]
            if columns is None:
                late = swapped(after(other, near), 1, slabs)
                theirs = after(theirs, got)
                columns = joined(where, theirs, swapped(theirs, 1, slabs))
            terms = [(own, (0, at)), (late, (0, at))] + [(block, (0, 0)) for block in got]
            mine = squares(width, terms)
            squared[n] = turned(mine, 1, batches)
            if n == ORDER[0]:
                kept = picked(where, after(gram_inverse, near), point_order, 0)
            pending = [links[p][0] if step else squared[p] for p, step in HOLD[n]]
            if pending:
                kept = after(kept, pending)
            share = shares(kept, columns, mine, squared[n])
            kept = after(kept, share[0])
            pieces[n], links[n] = combined(share, batches)
        fitted = [pieces[n] for n in range(len(WIDTHS))]
    else:
        tiles = fetched(points, blocks, block_of, live, 2 * REACH + 1)
        kept = picked(where, gram_inverse, point_order, 0)
        theirs = turned(picked(where, gram_inverse, point_order, 1), 1, batches)
        columns = joined(where, theirs, swapped(theirs, 1, slabs))
        terms = [(tiles, (REACH, 0, 0))] + [
            (passed_along(tiles[REACH + d], d, slabs), (0, 0)) for d in range(-REACH, REACH + 1) if d != 0
        ]
        mine = squares(cells, terms)
        fitted = [combined(shares(kept, columns, mine, turned(mine, 1, batches)), batches)[0]]
    return jnp.concatenate(fitted, axis=1)


def solution(mesh):
    in_specs = (
        P("grid", None, None, None),
        P("grid", None, "pts"),
        P("grid", None, "pts"),
        P("grid", None),
        P(),
        P("pts", None),
    )
    out_specs = P("pts", "grid")
    return jax.shard_map(
        on_device, mesh=mesh, in_specs=in_specs, out_specs=out_specs, check_vma=False
    )
```

```python
import functools

import jax
import jax.numpy as jnp
from jax import lax
from jax.experimental import pallas as pl
from jax.experimental.pallas import tpu as pltpu
from jax.sharding import PartitionSpec as P

REACH = 3
F32 = jnp.float32
WIDTHS = (128, 128, 128, 128)
ORDER = (0, 1, 2, 3)
HOLD = {0: (), 1: (), 2: ((0, 1),), 3: ((1, 1),)}
AFTER = ((), (), (('got', 0),), (('got', 1), ('squared', 0)))


def lasting(us):
    return pl.CostEstimate(flops=int(us * 1e9), bytes_accessed=int(us * 3e6), transcendentals=0)


CHUNKS = 4


def product(points_ref, block):
    return lax.dot_general(points_ref[...], block, (((0,), (0,)), ((), ())), preferred_element_type=F32)


def stream(block_of, live, points_ref, blocks_hbm, slots, done, base, count, emit):
    rows = slots.shape[1] // CHUNKS

    def copies(n):
        return [
            pltpu.make_async_copy(
                blocks_hbm.at[block_of[base + n], pl.ds(c * rows, rows)],
                slots.at[n % 2, pl.ds(c * rows, rows)],
                done.at[n % 2, c],
            )
            for c in range(CHUNKS)
        ]

    def start(n):
        @pl.when(live[base + n] != 0)
        def _():
            for copy in copies(n):
                copy.start()

    start(0)
    for n in range(count):

        @pl.when(live[base + n] != 0)
        def _(n=n):
            for copy in copies(n):
                copy.wait()

        if n + 1 < count:
            start(n + 1)

        @pl.when(live[base + n] != 0)
        def _(n=n):
            emit(n, product(points_ref, slots[n % 2]))

        @pl.when(live[base + n] == 0)
        def _(n=n):
            emit(n, None)


def fetched_kernel(count, block_of, live, points_ref, blocks_hbm, out_ref, slots, done):
    def emit(n, term):
        out_ref[n] = jnp.zeros(out_ref.shape[1:], F32) if term is None else term

    stream(block_of, live, points_ref, blocks_hbm, slots, done, 0, count, emit)


HBM = pl.BlockSpec(memory_space=pltpu.HBM)
SMEM = pl.BlockSpec(memory_space=pltpu.SMEM)
VMEM = pl.BlockSpec(memory_space=pltpu.VMEM)


def slots_for(blocks):
    return [pltpu.VMEM((2, *blocks.shape[1:]), blocks.dtype), pltpu.SemaphoreType.DMA((2, CHUNKS))]


def params(mib):
    return pltpu.CompilerParams(vmem_limit_bytes=mib << 20)


def fetched(points, blocks, block_of, live, count):
    orbs, batch = points.shape
    cells = blocks.shape[2]
    return pl.pallas_call(
        functools.partial(fetched_kernel, count),
        in_specs=[SMEM, SMEM, VMEM, pl.BlockSpec(memory_space=pltpu.HBM)],
        out_specs=VMEM,
        out_shape=jax.ShapeDtypeStruct((count, batch, cells), F32),
        scratch_shapes=slots_for(blocks),
        compiler_params=params(10),
        cost_estimate=lasting(2.5 * count),
        name="fetched",
    )(block_of, live, in_vmem(points), blocks)


def held_kernel(base, block_of, live, points_ref, blocks_hbm, *refs):
    *outs, slots, done = refs

    def emit(n, term):
        outs[n][...] = jnp.zeros(outs[n].shape, F32) if term is None else term

    stream(block_of, live, points_ref, blocks_hbm, slots, done, base, len(outs), emit)


def held(points, blocks, block_of, live, base, count):
    batch, cells = points.shape[1], blocks.shape[2]
    return pl.pallas_call(
        functools.partial(held_kernel, base),
        in_specs=[SMEM, SMEM, VMEM, HBM],
        out_specs=[VMEM] * count,
        out_shape=[jax.ShapeDtypeStruct((batch, cells), F32)] * count,
        scratch_shapes=slots_for(blocks),
        compiler_params=params(10),
        cost_estimate=lasting(2.0 * count),
        name="held",
    )(block_of, live, in_vmem(points), blocks)


def near_kernel(base, widths, block_of, live, points_ref, blocks_hbm, came_ref, *refs):
    *outs, slots, done = refs
    pieces = len(widths)

    def put(n, value):
        start = 0
        for out, width in zip(outs[n * pieces : (n + 1) * pieces], widths):
            out[...] = value[:, start : start + width]
            start += width

    put(2, came_ref[2])

    def emit(n, term):
        put(n, came_ref[n] if term is None else term + came_ref[n])

    stream(block_of, live, points_ref, blocks_hbm, slots, done, base, 2, emit)


def near_sums(points, blocks, block_of, live, base, came, widths):
    batch = points.shape[1]
    return pl.pallas_call(
        functools.partial(near_kernel, base, widths),
        in_specs=[SMEM, SMEM, VMEM, HBM, VMEM],
        scratch_shapes=slots_for(blocks),
        out_specs=[pl.BlockSpec((batch, width), lambda i: (0, 0)) for _ in range(3) for width in widths],
        out_shape=[pltpu.HBM((batch, width), F32) for _ in range(3) for width in widths],
        grid=(1,),
        compiler_params=params(16),
        cost_estimate=lasting(5.0),
        name="near_sums",
    )(block_of, live, in_vmem(points), blocks, in_vmem(came))


def in_vmem(array):
    return pltpu.with_memory_space_constraint(array, pltpu.VMEM)


def picked_kernel(where, order_ref, gram_ref, out_ref):
    del where
    rows = lax.broadcasted_iota(jnp.int32, (gram_ref.shape[1], order_ref.shape[1]), 0)
    chosen = (rows == order_ref[...]).astype(gram_ref.dtype)
    out_ref[...] = jnp.dot(gram_ref[...], chosen, preferred_element_type=F32).astype(out_ref.dtype)


def picked(where, gram, point_order, given):
    batch, points = gram.shape
    rows, span = batch // 2 if given else batch, 256
    per = batch // span

    def turn(i, where):
        return 0, (where[0] ^ (2 * lax.div(i, per) + given)) * per + lax.rem(i, per)

    return pl.pallas_call(
        picked_kernel,
        grid_spec=pltpu.PrefetchScalarGridSpec(
            num_scalar_prefetch=1,
            grid=(points // 2 // span,),
            in_specs=[
                pl.BlockSpec((1, span), turn),
                pl.BlockSpec(
                    (rows, points), lambda i, where: (where[1] if given else 0, 0), pipeline_mode=pl.Buffered(1)
                ),
            ],
            out_specs=pl.BlockSpec((rows, span), lambda i, where: (0, i)),
        ),
        out_shape=jax.ShapeDtypeStruct((rows, points // 2), F32 if given else gram.dtype),
        compiler_params=params(12),
        cost_estimate=lasting(3.0),
        name="picked",
    )(where, point_order[None, :], gram)


def joined_kernel(where, mine_ref, other_ref, out_ref):
    rows = mine_ref.shape[0]

    @pl.when(where[1] == 0)
    def _():
        out_ref[:rows] = mine_ref[...].astype(out_ref.dtype)
        out_ref[rows:] = other_ref[...].astype(out_ref.dtype)

    @pl.when(where[1] != 0)
    def _():
        out_ref[rows:] = mine_ref[...].astype(out_ref.dtype)
        out_ref[:rows] = other_ref[...].astype(out_ref.dtype)


def joined(where, mine, other):
    rows, columns = mine.shape
    return pl.pallas_call(
        joined_kernel,
        in_specs=[SMEM, VMEM, VMEM],
        out_specs=VMEM,
        out_shape=jax.ShapeDtypeStruct((2 * rows, columns), jnp.bfloat16),
        compiler_params=params(8),
        cost_estimate=lasting(1.5),
        name="joined",
    )(where, mine, other)


def squares_kernel(*refs):
    field = refs[0][...]
    for term in refs[1:-1]:
        field = field + term[...]
    refs[-1][...] = (field * field).astype(jnp.bfloat16).astype(F32)


def squares(width, terms):
    batch = terms[0][0].shape[-2]
    in_specs = []
    for array, at in terms:
        lead = (pl.Squeezed(),) * (array.ndim - 2)
        in_specs.append(pl.BlockSpec((*lead, batch, width), lambda i, at=at: at))
    return pl.pallas_call(
        squares_kernel,
        grid=(1,),
        in_specs=in_specs,
        out_specs=pl.BlockSpec((batch, width), lambda i: (0, 0)),
        out_shape=jax.ShapeDtypeStruct((batch, width), F32),
        compiler_params=params(8),
        cost_estimate=lasting(1.5),
        name="squares",
    )(*[array for array, _ in terms])


def shares_kernel(kept_ref, joined_ref, own_ref, came_ref, *outs):
    own, came = own_ref[...].astype(kept_ref.dtype), came_ref[...].astype(kept_ref.dtype)
    batch = own.shape[0]
    for n, out in enumerate(outs):
        cut = slice(n * batch, (n + 1) * batch)
        out[...] = lax.dot_general(
            kept_ref[:, cut], own, (((0,), (0,)), ((), ())), preferred_element_type=F32
        ) + lax.dot_general(joined_ref[:, cut], came, (((0,), (0,)), ((), ())), preferred_element_type=F32)


def shares(kept, joined, own, came):
    batch, width = own.shape
    count = kept.shape[1] // batch
    return pl.pallas_call(
        shares_kernel,
        in_specs=[VMEM] * 4,
        out_specs=[VMEM] * count,
        out_shape=[jax.ShapeDtypeStruct((batch, width), F32)] * count,
        compiler_params=params(8),
        cost_estimate=lasting(2.0),
        name="shares",
    )(kept, joined, own, came)


def swapped(block, mask, count):
    return lax.ppermute(block, "grid", [(i, i ^ mask) for i in range(count)])


def passed_along(block, distance, count):
    return lax.ppermute(block, "grid", [((i - distance) % count, i) for i in range(count)])


def turned(block, distance, count):
    return lax.ppermute(block, "pts", [(i, i ^ distance) for i in range(count)])


def combined(share, batches):
    kept, links = list(share), []
    distance = 2
    while distance < batches:
        sent, kept = kept[1::2], kept[0::2]
        came = turned(jnp.stack(sent) if len(sent) > 1 else sent[0][None], distance, batches)
        links.append(came)
        kept = [block + came[n] for n, block in enumerate(kept)]
        distance *= 2
    return kept[0].astype(jnp.bfloat16), links


def after(value, *others):
    return lax.optimization_barrier((value, *others))[0]


def on_device(phi_blocks, phi_points, tile_mask, support, point_order, gram_inverse):
    slabs, batches = lax.axis_size("grid"), lax.axis_size("pts")
    own_slab, own_batch = lax.axis_index("grid"), lax.axis_index("pts")
    blocks = pltpu.with_memory_space_constraint(phi_blocks[0], pltpu.HBM)
    cube = slabs == 8
    if cube:
        targets = own_slab ^ jnp.array([3, 7, 5, 0, 1, 2, 6, 0] + [0] * 8, jnp.int32)
    else:
        targets = (own_slab + jnp.array([d % slabs for d in range(-REACH, REACH + 1)] + [0] * 9, jnp.int32)) % slabs
    match = targets[:, None] == support[0][None, :]
    block_of = jnp.sum(jnp.where(match, jnp.arange(support.shape[1], dtype=jnp.int32)[None, :], 0), axis=1)
    live = jnp.sum(jnp.where(match, tile_mask[0, :, 0][None, :], 0), axis=1)
    where = jnp.stack([own_batch, own_slab & 1]).astype(jnp.int32)
    cells = phi_blocks.shape[-1]
    points = phi_points[0]
    if cube:
        away = fetched(points, blocks, block_of, live, 3)
        came = swapped(away, 1, slabs)
        own, other = held(after(points, away), blocks, block_of, live, 3, 2)
        theirs = turned(picked(where, after(gram_inverse, own), point_order, 1), 1, batches)
        near = near_sums(after(points, own), blocks, block_of, live, 5, came, WIDTHS)
        pieces, links, gots, squared = {}, {}, {}, {}
        columns = None
        for n in ORDER:
            width = WIDTHS[n]
            at = sum(WIDTHS[:n]) // width
            sums = [near[place * len(WIDTHS) + n] for place in range(3)]
            if n == ORDER[1]:
                sums = after(sums, late)
            if AFTER[n]:
                sums = after(sums, [{"got": gots, "squared": squared, "sum": links}[kind][p] for kind, p in AFTER[n]])
            got = gots[n] = [swapped(block, mask, slabs) for block, mask in zip(sums, (2, 6, 4))]
            if columns is None:
                late = swapped(after(other, near), 1, slabs)
                theirs = after(theirs, got)
                columns = joined(where, theirs, swapped(theirs, 1, slabs))
            terms = [(own, (0, at)), (late, (0, at))] + [(block, (0, 0)) for block in got]
            mine = squares(width, terms)
            squared[n] = turned(mine, 1, batches)
            if n == ORDER[0]:
                kept = picked(where, after(gram_inverse, near), point_order, 0)
            pending = [links[p][0] if step else squared[p] for p, step in HOLD[n]]
            if pending:
                kept = after(kept, pending)
            share = shares(kept, columns, mine, squared[n])
            kept = after(kept, share[0])
            pieces[n], links[n] = combined(share, batches)
        fitted = [pieces[n] for n in range(len(WIDTHS))]
    else:
        tiles = fetched(points, blocks, block_of, live, 2 * REACH + 1)
        kept = picked(where, gram_inverse, point_order, 0)
        theirs = turned(picked(where, gram_inverse, point_order, 1), 1, batches)
        columns = joined(where, theirs, swapped(theirs, 1, slabs))
        terms = [(tiles, (REACH, 0, 0))] + [
            (passed_along(tiles[REACH + d], d, slabs), (0, 0)) for d in range(-REACH, REACH + 1) if d != 0
        ]
        mine = squares(cells, terms)
        fitted = [combined(shares(kept, columns, mine, turned(mine, 1, batches)), batches)[0]]
    return jnp.concatenate(fitted, axis=1)


def solution(mesh):
    in_specs = (
        P("grid", None, None, None),
        P("grid", None, "pts"),
        P("grid", None, "pts"),
        P("grid", None),
        P(),
        P("pts", None),
    )
    out_specs = P("pts", "grid")
    return jax.shard_map(
        on_device, mesh=mesh, in_specs=in_specs, out_specs=out_specs, check_vma=False
    )
```
